32 devices in a mesh: tenant: 8 (over z, core), row: 4 (over y, x).
Axes of the slice: x: 2, y: 2, z: 4, core: 2. Of those that a mesh axis runs over, the one named last changes fastest.
Arguments:
- b_factors: float32 [64, 16, 8192], P('tenant', None, 'row'), may hold values from -6 to 6
- a_factors: float32 [64, 16, 8192], P('tenant', None, 'row'), may hold values from -6 to 6
- u_start: float32 [8192, 256], P('row'), may hold values from -0.0625 to 0.0625
- v_start: float32 [8192, 256], P('row'), may hold values from -0.0625 to 0.0625
Outputs:
- u_scaled: float32 [8192, 256], P('row')
- v_scaled: float32 [8192, 256], P('row')
- core_left: float32 [64, 16, 256], P('tenant')
- core_right: float32 [64, 16, 256], P('tenant')
The draws below stay inside these ranges and needn't reach their ends.
All inputs are finite; a program needn't handle non-finite values.
Results may differ from the reference program's by a relative error of at most 0.0003.
Values sent between devices are 32-bit elements; how exact they have to be, the bound alone decides.
A program may use at most 64 MiB of HBM per device.

```python
import math
import jax
import jax.numpy as jnp
from jax import lax

D = 8192
K = 256
R = 16
SWEEPS = 1
NT = 64


def steps_of(stream_key, dims, shards, low, largest):
    def one(axis_at, parts):
        heights = jax.random.uniform(jax.random.fold_in(jax.random.fold_in(stream_key, 6), axis_at), (parts,), jnp.float32, low / len(shards), largest / len(shards))
        return jnp.repeat(jnp.exp(heights), dims[axis_at] // parts).reshape((-1,) + (1,) * (len(dims) - axis_at - 1))

    level = one(*shards[0])
    for cut in shards[1:]:
        level = level * one(*cut)
    return level


def noise(stream_key, shape, scale, limit, cuts=(), kind=jnp.bfloat16):
    drawn = scale * jax.random.normal(stream_key, shape, jnp.float32)
    if cuts:
        drawn = drawn * steps_of(stream_key, shape, cuts, -0.22, 0.18)
    return jnp.clip(drawn, -limit, limit).astype(kind)


def setup_inputs(seed: int = 0) -> dict:
    streams_of = jax.random.split(jax.random.key(seed), 5)
    return {
        "b_factors": noise(streams_of[0], (NT, R, D), 1.0, 6.0, ((0, 8), (2, 4)), jnp.float32),
        "a_factors": noise(streams_of[1], (NT, R, D), 1.0, 6.0, ((0, 8), (2, 4)), jnp.float32),
        "u_start": noise(streams_of[2], (D, K), D ** -0.5, 0.0625, ((0, 4),), jnp.float32),
        "v_start": noise(streams_of[3], (D, K), D ** -0.5, 0.0625, ((0, 4),), jnp.float32),
    }


HIGH = lax.Precision.HIGHEST

def project(factors, basis):
    return jnp.einsum('trd,dk->trk', factors, basis, precision=HIGH)

def orthonormal(matrix):
    gram = jnp.dot(matrix.T, matrix, precision=HIGH)
    lower = jnp.linalg.cholesky(gram)
    return lax.linalg.triangular_solve(lower, matrix, left_side=False, lower=True, transpose_a=True)

def reference(b_factors, a_factors, u_start, v_start):
    left = project(b_factors, u_start)
    right = project(a_factors, v_start)
    basis_u = u_start
    basis_v = v_start
    for sweep in range(SWEEPS):
        weight = jnp.einsum('trk,tsk->trs', right, right, precision=HIGH)
        coeffs = jnp.einsum('trs,tsk->trk', weight, left, precision=HIGH)
        basis_u = orthonormal(jnp.einsum('trd,trk->dk', b_factors, coeffs, precision=HIGH))
        left = project(b_factors, basis_u)
        weight = jnp.einsum('trk,tsk->trs', left, left, precision=HIGH)
        coeffs = jnp.einsum('trs,tsk->trk', weight, right, precision=HIGH)
        basis_v = orthonormal(jnp.einsum('trd,trk->dk', a_factors, coeffs, precision=HIGH))
        right = project(a_factors, basis_v)
    scale = math.sqrt(D)
    return (basis_u * scale, basis_v * scale, left, right)
```

```python
import functools
import math

import jax
import jax.numpy as jnp
from jax import lax
from jax.experimental import pallas as pl
from jax.experimental.pallas import tpu as pltpu
from jax.sharding import PartitionSpec as P

HIGH = lax.Precision.HIGHEST
MESH = pl.DeviceIdType.MESH
VMEM = pl.BlockSpec(memory_space=pltpu.VMEM)
LANES = 128
BLK = 64


def mm(x, y, cx, cy):
    return lax.dot_general(x, y, (((cx,), (cy,)), ((), ())), precision=HIGH, preferred_element_type=jnp.float32)


def remote(src, dst, send, recv, device):
    return pltpu.make_async_remote_copy(
        src_ref=src, dst_ref=dst, send_sem=send, recv_sem=recv, device_id=device, device_id_type=MESH)


def signal(device):
    pl.semaphore_signal(pltpu.get_barrier_semaphore(), inc=1, device_id=device, device_id_type=MESH)


def bits_of(n_row):
    bits = n_row.bit_length() - 1
    assert 1 << bits == n_row
    return bits


def row_partner(bit):
    row = lax.axis_index("row")
    return row + (1 << bit) - 2 * (1 << bit) * (lax.rem(row // (1 << bit), 2))


def row_sum(bits, acc, got, send, recv):
    half = acc.shape[1] // 2

    def copy(step, part):
        bit = (step + part) % bits
        rows = pl.ds(part * half, half)
        return remote(acc.at[step, rows], got.at[step, rows], send.at[step, part], recv.at[step, part],
                      {"row": row_partner(bit)})

    for part in range(2):
        copy(0, part).start()
    for step in range(bits):
        for part in range(2):
            rows = pl.ds(part * half, half)
            copy(step, part).wait_recv()
            acc[step + 1, rows, :] = acc[step, rows, :] + got[step, rows, :]
            if step + 1 < bits:
                copy(step + 1, part).start()
    for step in range(bits):
        for part in range(2):
            copy(step, part).wait_send()


def start_kernel(bits, b_ref, a_ref, u_ref, v_ref, out_ref, acc, got, send, recv):
    for bit in range(bits):
        signal({"row": row_partner(bit)})
    rows, width = b_ref.shape
    tile = 512 if width % 512 == 0 else width
    acc[0] = jnp.zeros_like(acc[0])

    def step(i, _):
        cols = pl.ds(pl.multiple_of(i * tile, tile), tile)
        acc[0, :rows, :] += mm(b_ref[:, cols], u_ref[cols, :], 1, 0)
        acc[0, rows:, :] += mm(a_ref[:, cols], v_ref[cols, :], 1, 0)
        return 0

    lax.fori_loop(0, width // tile, step, 0)
    pl.semaphore_wait(pltpu.get_barrier_semaphore(), bits)
    row_sum(bits, acc, got, send, recv)
    out_ref[...] = acc[bits]


def start(bits, b, a, u, v):
    rows, k = b.shape[0], u.shape[1]
    return pl.pallas_call(
        functools.partial(start_kernel, bits),
        out_shape=jax.ShapeDtypeStruct((2 * rows, k), jnp.float32),
        in_specs=[VMEM] * 4,
        out_specs=VMEM,
        scratch_shapes=[
            pltpu.VMEM((bits + 1, 2 * rows, k), jnp.float32),
            pltpu.VMEM((bits, 2 * rows, k), jnp.float32),
            pltpu.SemaphoreType.DMA((bits, 2)),
            pltpu.SemaphoreType.DMA((bits, 2)),
        ],
        compiler_params=pltpu.CompilerParams(collective_id=0, has_side_effects=True),
    )(b, a, u, v)


def refresh_kernel(bits, chain, rank, f_ref, x_ref, y_ref, m_ref, s_ref, other, pair, up, got, acc, rgot, coeff,
                   pair_send, pair_recv, in_send, recv, out_send, fin_send, fin_recv, row_send, row_recv):
    tenant = lax.axis_index("tenant")
    core = lax.rem(tenant, 2)
    place = tenant // 2
    nch = other.shape[0]
    lower = (place < chain // 2).astype(jnp.int32)
    toward = 2 * lower - 1
    mate = {"tenant": tenant + 1 - 2 * core}
    inner = {"tenant": tenant + 2 * toward}
    dist = lower * (chain // 2 - 1 - place) + (1 - lower) * (place - chain // 2)
    mid = (dist == 0).astype(jnp.int32)
    is_end = dist == chain // 2 - 1
    outer = {"tenant": jnp.where(is_end, tenant, tenant - 2 * toward)}

    signal(mate)
    signal(inner)
    for bit in range(bits):
        signal({"row": row_partner(bit)})

    @pl.when(jnp.logical_not(is_end))
    def _():
        signal(outer)

    rows, width = f_ref.shape
    half = width // 2
    tile = other.shape[1]
    weight = mm(x_ref[...], x_ref[...], 1, 1)
    same = lax.broadcasted_iota(jnp.int32, weight.shape, 0) // rank == lax.broadcasted_iota(
        jnp.int32, weight.shape, 1) // rank
    coeff[...] = mm(jnp.where(same, weight, 0.0), y_ref[...], 1, 0)
    pl.semaphore_wait(pltpu.get_barrier_semaphore(), 3 + bits - is_end.astype(jnp.int32))

    def rows_of(side, ch):
        return pl.ds(pl.multiple_of(side * half + ch * tile, tile), tile)

    def term(side, ch):
        return mm(f_ref[:, rows_of(side, ch)], coeff[...], 0, 0)

    def pair_copy(ch):
        return remote(other.at[ch], pair.at[ch], pair_send.at[ch], pair_recv.at[ch], mate)

    def in_copy(ch, slot):
        return remote(up.at[ch], got.at[slot, ch], in_send.at[ch], recv.at[slot, ch], inner)

    def out_copy(ch):
        mine = m_ref.at[rows_of(core, ch)]
        return remote(mine, got.at[1, ch], out_send.at[ch], recv.at[1, ch], outer)

    def fin_copy(side, ch):
        part = m_ref.at[rows_of(side, ch)]
        return remote(part, part, fin_send.at[ch], fin_recv.at[ch], mate)

    acc[0] = jnp.zeros_like(acc[0])

    def first(ch, _):
        other[ch] = term(1 - core, ch)
        pair_copy(ch).start()
        return 0

    lax.fori_loop(0, nch, first, 0)

    def gather_up(ch):
        up[ch] = term(core, ch)
        pair_copy(ch).wait_recv()
        up[ch] += pair[ch]

        @pl.when(jnp.logical_not(is_end))
        def _():
            in_copy(ch, 0).wait_recv()
            up[ch] += got[0, ch]

        in_copy(ch, mid).start()

    def accumulate(ch):
        fin_copy(1 - core, ch).wait_recv()
        for side in range(2):
            block = m_ref[rows_of(side, ch), :]
            acc[0, :rows, :] += mm(f_ref[:, rows_of(side, ch)], block, 1, 0)
            acc[0, rows:, :] += mm(block, block, 0, 0)

    def settle(ch):
        in_copy(ch, 1).wait_recv()

        @pl.when(mid == 1)
        def _():
            m_ref[rows_of(core, ch), :] = up[ch] + got[1, ch]

        @pl.when(mid == 0)
        def _():
            m_ref[rows_of(core, ch), :] = got[1, ch]

        @pl.when(jnp.logical_not(is_end))
        def _():
            out_copy(ch).start()

        fin_copy(core, ch).start()

        @pl.when(ch > 0)
        def _():
            accumulate(ch - 1)

    lag = 1 + 4 * dist

    def step(i, _):
        @pl.when(i < nch)
        def _():
            gather_up(i)

        @pl.when(jnp.logical_and(i >= lag, i < nch + lag))
        def _():
            settle(i - lag)

        return 0

    lax.fori_loop(0, nch + 1 + 4 * (chain // 2 - 1), step, 0)
    accumulate(nch - 1)
    row_sum(bits, acc, rgot, row_send, row_recv)
    s_ref[...] = acc[bits]

    def drain(ch, _):
        pair_copy(ch).wait_send()
        in_copy(ch, mid).wait_send()
        fin_copy(core, ch).wait_send()

        @pl.when(jnp.logical_not(is_end))
        def _():
            out_copy(ch).wait_send()

        return 0

    lax.fori_loop(0, nch, drain, 0)


def refresh(bits, chain, rank, f, x, y):
    rows, width = f.shape
    k = x.shape[1]
    tile = min(LANES, width // 2)
    nch = width // 2 // tile
    f32 = jnp.float32
    dma = pltpu.SemaphoreType.DMA
    return pl.pallas_call(
        functools.partial(refresh_kernel, bits, chain, rank),
        out_shape=(jax.ShapeDtypeStruct((width, k), f32), jax.ShapeDtypeStruct((rows + k, k), f32)),
        in_specs=[VMEM] * 3,
        out_specs=(VMEM, VMEM),
        scratch_shapes=[
            pltpu.VMEM((nch, tile, k), f32),
            pltpu.VMEM((nch, tile, k), f32),
            pltpu.VMEM((nch, tile, k), f32),
            pltpu.VMEM((2, nch, tile, k), f32),
            pltpu.VMEM((bits + 1, rows + k, k), f32),
            pltpu.VMEM((bits, rows + k, k), f32),
            pltpu.VMEM((rows, k), f32),
            dma((nch,)), dma((nch,)), dma((nch,)), dma((2, nch)), dma((nch,)), dma((nch,)), dma((nch,)),
            dma((bits, 2)), dma((bits, 2)),
        ],
        compiler_params=pltpu.CompilerParams(collective_id=1, has_side_effects=True),
    )(f, x, y)


def factor_block(block):
    n = block.shape[0]
    eye = (lax.broadcasted_iota(jnp.int32, (n, n), 0) == lax.broadcasted_iota(jnp.int32, (n, n), 1)).astype(block.dtype)
    full = jnp.concatenate([block, eye], axis=1)
    groups = [full[8 * g:8 * g + 8, :] for g in range(n // 8)]
    sub = lax.broadcasted_iota(jnp.int32, (8, 1), 0)
    for j in range(n):
        g, s = j // 8, j % 8
        row = groups[g][s:s + 1, :]
        inv = 1.0 / row[:, j:j + 1]
        scaled = row * inv
        for h in range(g, n // 8):
            col = groups[h][:, j:j + 1]
            if h == g:
                col = jnp.where(sub > s, col, 0.0)
            groups[h] = groups[h] - col * scaled
    full = jnp.concatenate(groups, axis=0)
    diag = jnp.sum(full[:, :n] * eye, axis=1, keepdims=True)
    return full[:, n:] * lax.rsqrt(diag)


def factor_kernel(s_ref, inv_ref, left_ref, tab):
    k = inv_ref.shape[0]
    rows = left_ref.shape[0]
    tab[:, :k] = s_ref[rows:, :]
    tab[:, k:] = (lax.broadcasted_iota(jnp.int32, (k, k), 0) == lax.broadcasted_iota(
        jnp.int32, (k, k), 1)).astype(jnp.float32)
    for at in range(0, k, BLK):
        end = at + BLK
        small = factor_block(tab[at:end, at:end])
        done = mm(small, tab[at:end, :], 1, 0)
        tab[at:end, :] = done
        if end < k:
            tab[end:, :] -= mm(done[:, end:k], done, 0, 0)
    inv_ref[...] = tab[:, k:]
    left_ref[...] = mm(s_ref[:rows, :], tab[:, k:], 1, 1)


def factor(s):
    k = s.shape[1]
    rows = s.shape[0] - k
    return pl.pallas_call(
        factor_kernel,
        out_shape=(jax.ShapeDtypeStruct((k, k), jnp.float32), jax.ShapeDtypeStruct((rows, k), jnp.float32)),
        in_specs=[VMEM],
        out_specs=(VMEM, VMEM),
        scratch_shapes=[pltpu.VMEM((k, 2 * k), jnp.float32)],
    )(s)


def local(mesh_shape, b_factors, a_factors, u_start, v_start):
    nt, rank, width = b_factors.shape
    rows = nt * rank
    k = u_start.shape[1]
    bits = bits_of(mesh_shape["row"])
    chain = mesh_shape["tenant"] // 2
    b = b_factors.reshape(rows, width)
    a = a_factors.reshape(rows, width)
    both = start(bits, b, a, u_start, v_start)
    left, right = both[:rows], both[rows:]
    basis_u, sums = refresh(bits, chain, rank, b, right, left)
    inv_u, left = factor(sums)
    basis_v, sums = refresh(bits, chain, rank, a, left, right)
    inv_v, right = factor(sums)
    scale = math.sqrt(width * mesh_shape["row"])
    u = mm(basis_u, inv_u * scale, 1, 1)
    v = mm(basis_v, inv_v * scale, 1, 1)
    return u, v, left.reshape(nt, rank, k), right.reshape(nt, rank, k)


def solution(mesh):
    in_specs = (P("tenant", None, "row"), P("tenant", None, "row"), P("row", None), P("row", None))
    out_specs = (P("row", None), P("row", None), P("tenant", None, None), P("tenant", None, None))
    return jax.shard_map(functools.partial(local, dict(mesh.shape)), mesh=mesh, in_specs=in_specs,
                         out_specs=out_specs, check_vma=False)
```

```python
import functools
import math

import jax
import jax.numpy as jnp
from jax import lax
from jax.experimental import pallas as pl
from jax.experimental.pallas import tpu as pltpu
from jax.sharding import PartitionSpec as P

HIGH = lax.Precision.HIGHEST
MESH = pl.DeviceIdType.MESH
VMEM = pl.BlockSpec(memory_space=pltpu.VMEM)
LANES = 128
BLK = 64


def mm(x, y, cx, cy):
    return lax.dot_general(x, y, (((cx,), (cy,)), ((), ())), precision=HIGH, preferred_element_type=jnp.float32)


def split(x):
    top = x.astype(jnp.bfloat16)
    return top, (x - top.astype(jnp.float32)).astype(jnp.bfloat16)


def mm3(x, y, cx, cy):
    (xt, xl), (yt, yl) = split(x), split(y)
    dot = functools.partial(lax.dot_general, dimension_numbers=(((cx,), (cy,)), ((), ())),
                            preferred_element_type=jnp.float32)
    return dot(xt, yt) + (dot(xt, yl) + dot(xl, yt))


def remote(src, dst, send, recv, device):
    return pltpu.make_async_remote_copy(
        src_ref=src, dst_ref=dst, send_sem=send, recv_sem=recv, device_id=device, device_id_type=MESH)


def signal(device):
    pl.semaphore_signal(pltpu.get_barrier_semaphore(), inc=1, device_id=device, device_id_type=MESH)


def bits_of(n_row):
    bits = n_row.bit_length() - 1
    assert 1 << bits == n_row
    return bits


def row_partner(bit):
    row = lax.axis_index("row")
    return row + (1 << bit) - 2 * (1 << bit) * (lax.rem(row // (1 << bit), 2))


def row_sum(bits, acc, got, send, recv):
    half = acc.shape[1] // 2

    def copy(step, part):
        bit = (step + part) % bits
        rows = pl.ds(part * half, half)
        return remote(acc.at[step, rows], got.at[step, rows], send.at[step, part], recv.at[step, part],
                      {"row": row_partner(bit)})

    for part in range(2):
        copy(0, part).start()
    for step in range(bits):
        for part in range(2):
            rows = pl.ds(part * half, half)
            copy(step, part).wait_recv()
            acc[step + 1, rows, :] = acc[step, rows, :] + got[step, rows, :]
            if step + 1 < bits:
                copy(step + 1, part).start()
    for step in range(bits):
        for part in range(2):
            copy(step, part).wait_send()


def start_kernel(bits, b_ref, a_ref, u_ref, v_ref, out_ref, acc, got, send, recv):
    for bit in range(bits):
        signal({"row": row_partner(bit)})
    rows, width = b_ref.shape
    tile = 512 if width % 512 == 0 else width
    acc[0] = jnp.zeros_like(acc[0])

    def step(i, _):
        cols = pl.ds(pl.multiple_of(i * tile, tile), tile)
        acc[0, :rows, :] += mm3(b_ref[:, cols], u_ref[cols, :], 1, 0)
        acc[0, rows:, :] += mm3(a_ref[:, cols], v_ref[cols, :], 1, 0)
        return 0

    lax.fori_loop(0, width // tile, step, 0)
    pl.semaphore_wait(pltpu.get_barrier_semaphore(), bits)
    row_sum(bits, acc, got, send, recv)
    out_ref[...] = acc[bits]


def start(bits, b, a, u, v):
    rows, k = b.shape[0], u.shape[1]
    return pl.pallas_call(
        functools.partial(start_kernel, bits),
        out_shape=jax.ShapeDtypeStruct((2 * rows, k), jnp.float32),
        in_specs=[VMEM] * 4,
        out_specs=VMEM,
        scratch_shapes=[
            pltpu.VMEM((bits + 1, 2 * rows, k), jnp.float32),
            pltpu.VMEM((bits, 2 * rows, k), jnp.float32),
            pltpu.SemaphoreType.DMA((bits, 2)),
            pltpu.SemaphoreType.DMA((bits, 2)),
        ],
        compiler_params=pltpu.CompilerParams(collective_id=0, has_side_effects=True),
    )(b, a, u, v)


def refresh_kernel(bits, chain, rank, f_ref, x_ref, y_ref, m_ref, s_ref, other, pair, up, got, acc, rgot, coeff,
                   pair_send, pair_recv, in_send, recv, out_send, fin_send, fin_recv, row_send, row_recv, gram_send, gram_recv):
    tenant = lax.axis_index("tenant")
    core = lax.rem(tenant, 2)
    place = tenant // 2
    nch = other.shape[0]
    lower = (place < chain // 2).astype(jnp.int32)
    toward = 2 * lower - 1
    mate = {"tenant": tenant + 1 - 2 * core}
    inner = {"tenant": tenant + 2 * toward}
    dist = lower * (chain // 2 - 1 - place) + (1 - lower) * (place - chain // 2)
    mid = (dist == 0).astype(jnp.int32)
    is_end = dist == chain // 2 - 1
    outer = {"tenant": jnp.where(is_end, tenant, tenant - 2 * toward)}

    signal(mate)
    signal(inner)
    for bit in range(bits):
        signal({"row": row_partner(bit)})

    @pl.when(jnp.logical_not(is_end))
    def _():
        signal(outer)

    rows, width = f_ref.shape
    half = width // 2
    tile = other.shape[1]
    weight = mm(x_ref[...], x_ref[...], 1, 1)
    same = lax.broadcasted_iota(jnp.int32, weight.shape, 0) // rank == lax.broadcasted_iota(
        jnp.int32, weight.shape, 1) // rank
    coeff[...] = mm(jnp.where(same, weight, 0.0), y_ref[...], 1, 0)
    pl.semaphore_wait(pltpu.get_barrier_semaphore(), 3 + bits - is_end.astype(jnp.int32))

    def rows_of(side, ch):
        return pl.ds(pl.multiple_of(side * half + ch * tile, tile), tile)

    def term(side, ch):
        return mm3(f_ref[:, rows_of(side, ch)], coeff[...], 0, 0)

    def pair_copy(ch):
        return remote(other.at[ch], pair.at[ch], pair_send.at[ch], pair_recv.at[ch], mate)

    def in_copy(ch, slot):
        return remote(up.at[ch], got.at[slot, ch], in_send.at[ch], recv.at[slot, ch], inner)

    def out_copy(ch):
        mine = m_ref.at[rows_of(core, ch)]
        return remote(mine, got.at[1, ch], out_send.at[ch], recv.at[1, ch], outer)

    def fin_copy(side, ch):
        part = m_ref.at[rows_of(side, ch)]
        return remote(part, part, fin_send.at[ch], fin_recv.at[ch], mate)

    acc[0] = jnp.zeros_like(acc[0])

    def first(ch, _):
        other[ch] = term(1 - core, ch)
        pair_copy(ch).start()
        return 0

    lax.fori_loop(0, nch, first, 0)

    def gather_up(ch):
        up[ch] = term(core, ch)
        pair_copy(ch).wait_recv()
        up[ch] += pair[ch]

        @pl.when(jnp.logical_not(is_end))
        def _():
            in_copy(ch, 0).wait_recv()
            up[ch] += got[0, ch]

        in_copy(ch, mid).start()

    k = m_ref.shape[1]
    part = pl.ds(pl.multiple_of(core * (k // 2), k // 2), k // 2)

    def accumulate(ch):
        fin_copy(1 - core, ch).wait_recv()
        for side in range(2):
            block = m_ref[rows_of(side, ch), :]
            acc[0, :rows, :] += mm3(f_ref[:, rows_of(side, ch)], block, 1, 0)
            acc[0, rows:, :] += mm(m_ref[rows_of(side, ch), part], block, 0, 0)

    def settle(ch):
        in_copy(ch, 1).wait_recv()

        @pl.when(mid == 1)
        def _():
            m_ref[rows_of(core, ch), :] = up[ch] + got[1, ch]

        @pl.when(mid == 0)
        def _():
            m_ref[rows_of(core, ch), :] = got[1, ch]

        @pl.when(jnp.logical_not(is_end))
        def _():
            out_copy(ch).start()

        fin_copy(core, ch).start()

        @pl.when(ch > 0)
        def _():
            accumulate(ch - 1)

    lag = 1 + 4 * dist

    def step(i, _):
        @pl.when(i < nch)
        def _():
            gather_up(i)

        @pl.when(jnp.logical_and(i >= lag, i < nch + lag))
        def _():
            settle(i - lag)

        return 0

    lax.fori_loop(0, nch + 1 + 4 * (chain // 2 - 1), step, 0)
    accumulate(nch - 1)
    row_sum(bits, acc, rgot, row_send, row_recv)
    s_ref[:rows, :] = acc[bits, :rows, :]

    def gram_copy(side):
        here = s_ref.at[pl.ds(pl.multiple_of(rows + side * (k // 2), 8), k // 2)]
        return remote(here, here, gram_send, gram_recv, mate)

    s_ref[pl.ds(pl.multiple_of(rows + core * (k // 2), 8), k // 2), :] = acc[bits, rows:, :]
    gram_copy(core).start()

    def drain(ch, _):
        pair_copy(ch).wait_send()
        in_copy(ch, mid).wait_send()
        fin_copy(core, ch).wait_send()

        @pl.when(jnp.logical_not(is_end))
        def _():
            out_copy(ch).wait_send()

        return 0

    lax.fori_loop(0, nch, drain, 0)
    gram_copy(1 - core).wait_recv()
    gram_copy(core).wait_send()


def refresh(bits, chain, rank, f, x, y):
    rows, width = f.shape
    k = x.shape[1]
    tile = min(LANES, width // 2)
    nch = width // 2 // tile
    f32 = jnp.float32
    dma = pltpu.SemaphoreType.DMA
    return pl.pallas_call(
        functools.partial(refresh_kernel, bits, chain, rank),
        out_shape=(jax.ShapeDtypeStruct((width, k), f32), jax.ShapeDtypeStruct((rows + k, k), f32)),
        in_specs=[VMEM] * 3,
        out_specs=(VMEM, VMEM),
        scratch_shapes=[
            pltpu.VMEM((nch, tile, k), f32),
            pltpu.VMEM((nch, tile, k), f32),
            pltpu.VMEM((nch, tile, k), f32),
            pltpu.VMEM((2, nch, tile, k), f32),
            pltpu.VMEM((bits + 1, rows + k // 2, k), f32),
            pltpu.VMEM((bits, rows + k // 2, k), f32),
            pltpu.VMEM((rows, k), f32),
            dma((nch,)), dma((nch,)), dma((nch,)), dma((2, nch)), dma((nch,)), dma((nch,)), dma((nch,)),
            dma((bits, 2)), dma((bits, 2)), dma(()), dma(()),
        ],
        compiler_params=pltpu.CompilerParams(collective_id=1, has_side_effects=True),
    )(f, x, y)


def factor_block(block):
    n = block.shape[0]
    eye = (lax.broadcasted_iota(jnp.int32, (n, n), 0) == lax.broadcasted_iota(jnp.int32, (n, n), 1)).astype(block.dtype)
    full = jnp.concatenate([block, eye], axis=1)
    groups = [full[8 * g:8 * g + 8, :] for g in range(n // 8)]
    sub = lax.broadcasted_iota(jnp.int32, (8, 2 * n), 0)
    for g in range(n // 8):
        cols = [[jnp.broadcast_to(groups[h][:, 8 * g + c:8 * g + c + 1], (8, 2 * n)) for c in range(8)]
                for h in range(g, n // 8)]
        heads = [[cols[0][c][r:r + 1, :] for c in range(8)] for r in range(8)]
        lines = [groups[g][r:r + 1, :] for r in range(8)]
        invs = []
        for p in range(8):
            inv = 1.0 / heads[p][p]
            invs.append(inv)
            for r in range(p + 1, 8):
                factor = heads[r][p] * inv
                lines[r] = lines[r] - factor * lines[p]
                for c in range(p + 1, 8):
                    heads[r][c] = heads[r][c] - factor * heads[p][c]
        for h in range(g + 1, n // 8):
            col = cols[h - g]
            total = groups[h]
            for p in range(8):
                factor = col[p] * invs[p]
                total = total - factor * lines[p]
                for c in range(p + 1, 8):
                    col[c] = col[c] - factor * heads[p][c]
            groups[h] = total
        group = jnp.broadcast_to(lines[0], (8, 2 * n))
        for r in range(1, 8):
            group = jnp.where(sub == r, lines[r], group)
        groups[g] = group
    full = jnp.concatenate(groups, axis=0)
    diag = jnp.sum(full[:, :n] * eye, axis=1, keepdims=True)
    return full[:, n:] * lax.rsqrt(diag)


def factor_kernel(s_ref, inv_ref, left_ref, tab):
    k = inv_ref.shape[0]
    rows = left_ref.shape[0]
    tab[:, :k] = s_ref[rows:, :]
    tab[:, k:] = (lax.broadcasted_iota(jnp.int32, (k, k), 0) == lax.broadcasted_iota(
        jnp.int32, (k, k), 1)).astype(jnp.float32)
    for at in range(0, k, BLK):
        end = at + BLK
        small = factor_block(tab[at:end, at:end])
        done = mm(small, tab[at:end, :], 1, 0)
        tab[at:end, :] = done
        if end < k:
            tab[end:, :] -= mm(done[:, end:k], done, 0, 0)
    inv_ref[...] = tab[:, k:]
    left_ref[...] = mm(s_ref[:rows, :], tab[:, k:], 1, 1)


def factor(s):
    k = s.shape[1]
    rows = s.shape[0] - k
    return pl.pallas_call(
        factor_kernel,
        out_shape=(jax.ShapeDtypeStruct((k, k), jnp.float32), jax.ShapeDtypeStruct((rows, k), jnp.float32)),
        in_specs=[VMEM],
        out_specs=(VMEM, VMEM),
        scratch_shapes=[pltpu.VMEM((k, 2 * k), jnp.float32)],
    )(s)


def finish(basis, inv):
    return lax.dot_general(basis, inv, (((1,), (1,)), ((), ())), precision=lax.Precision.HIGH)


def local(mesh_shape, b_factors, a_factors, u_start, v_start):
    nt, rank, width = b_factors.shape
    rows = nt * rank
    k = u_start.shape[1]
    bits = bits_of(mesh_shape["row"])
    chain = mesh_shape["tenant"] // 2
    b = b_factors.reshape(rows, width)
    a = a_factors.reshape(rows, width)
    both = start(bits, b, a, u_start, v_start)
    left, right = both[:rows], both[rows:]
    basis_u, sums = refresh(bits, chain, rank, b, right, left)
    inv_u, left = factor(sums)
    basis_v, sums = refresh(bits, chain, rank, a, left, right)
    inv_v, right = factor(sums)
    scale = math.sqrt(width * mesh_shape["row"])
    u = finish(basis_u, inv_u * scale)
    v = finish(basis_v, inv_v * scale)
    return u, v, left.reshape(nt, rank, k), right.reshape(nt, rank, k)


def solution(mesh):
    in_specs = (P("tenant", None, "row"), P("tenant", None, "row"), P("row", None), P("row", None))
    out_specs = (P("row", None), P("row", None), P("tenant", None, None), P("tenant", None, None))
    return jax.shard_map(functools.partial(local, dict(mesh.shape)), mesh=mesh, in_specs=in_specs,
                         out_specs=out_specs, check_vma=False)
```

```python
import functools
import math

import jax
import jax.numpy as jnp
from jax import lax
from jax.experimental import pallas as pl
from jax.experimental.pallas import tpu as pltpu
from jax.sharding import PartitionSpec as P

HIGH = lax.Precision.HIGHEST
MESH = pl.DeviceIdType.MESH
VMEM = pl.BlockSpec(memory_space=pltpu.VMEM)
LANES = 128
BLK = 64


def mm(x, y, cx, cy):
    return lax.dot_general(x, y, (((cx,), (cy,)), ((), ())), precision=HIGH, preferred_element_type=jnp.float32)


def split(x):
    top = x.astype(jnp.bfloat16)
    return top, (x - top.astype(jnp.float32)).astype(jnp.bfloat16)


def mm3(x, y, cx, cy):
    (xt, xl), (yt, yl) = split(x), split(y)
    dot = functools.partial(lax.dot_general, dimension_numbers=(((cx,), (cy,)), ((), ())),
                            preferred_element_type=jnp.float32)
    return dot(xt, yt) + (dot(xt, yl) + dot(xl, yt))


def remote(src, dst, send, recv, device):
    return pltpu.make_async_remote_copy(
        src_ref=src, dst_ref=dst, send_sem=send, recv_sem=recv, device_id=device, device_id_type=MESH)


def signal(device):
    pl.semaphore_signal(pltpu.get_barrier_semaphore(), inc=1, device_id=device, device_id_type=MESH)


def bits_of(n_row):
    bits = n_row.bit_length() - 1
    assert 1 << bits == n_row
    return bits


def row_partner(bit):
    row = lax.axis_index("row")
    return row + (1 << bit) - 2 * (1 << bit) * (lax.rem(row // (1 << bit), 2))


def row_parts(bits, acc, got, send, recv, base, size):
    half = size // 2

    def copy(step, part):
        bit = (step + part) % bits
        rows = pl.ds(base + part * half, half)
        at = base // size
        return remote(acc.at[step, rows], got.at[step, rows], send.at[at, step, part], recv.at[at, step, part],
                      {"row": row_partner(bit)})

    def begin():
        for part in range(2):
            copy(0, part).start()

    def meet(step):
        for part in range(2):
            rows = pl.ds(base + part * half, half)
            copy(step, part).wait_recv()
            acc[step + 1, rows, :] = acc[step, rows, :] + got[step, rows, :]
            if step + 1 < bits:
                copy(step + 1, part).start()

    def end():
        for step in range(bits):
            for part in range(2):
                copy(step, part).wait_send()

    return begin, meet, end


def row_sum(bits, acc, got, send, recv):
    begin, meet, end = row_parts(bits, acc, got, send, recv, 0, acc.shape[1])
    begin()
    for step in range(bits):
        meet(step)
    end()


def start_kernel(bits, b_hbm, a_hbm, u_hbm, v_hbm, left_ref, right_ref, b_ref, a_ref, u_ref, v_ref, acc, got,
                 load, send, recv):
    pairs = ((b_hbm, b_ref), (u_hbm, u_ref), (a_hbm, a_ref), (v_hbm, v_ref))
    loads = [pltpu.make_async_copy(src, dst, load.at[i]) for i, (src, dst) in enumerate(pairs)]
    for copy in loads:
        copy.start()
    for bit in range(bits):
        signal({"row": row_partner(bit)})
    rows, width = b_ref.shape
    tile = 512 if width % 512 == 0 else width
    acc[0] = jnp.zeros_like(acc[0])
    parts = [row_parts(bits, acc, got, send, recv, side * rows, rows) for side in range(2)]
    for side, (factors, basis) in enumerate(((b_ref, u_ref), (a_ref, v_ref))):
        loads[2 * side].wait()
        loads[2 * side + 1].wait()

        def step(i, _, side=side, factors=factors, basis=basis):
            cols = pl.ds(pl.multiple_of(i * tile, tile), tile)
            acc[0, pl.ds(side * rows, rows), :] += mm3(factors[:, cols], basis[cols, :], 1, 0)
            return 0

        lax.fori_loop(0, width // tile, step, 0)
        if side == 0:
            pl.semaphore_wait(pltpu.get_barrier_semaphore(), bits)
        parts[side][0]()
    for step in range(bits):
        for side in range(2):
            parts[side][1](step)
    for side in range(2):
        parts[side][2]()
    left_ref[...] = acc[bits, :rows, :]
    right_ref[...] = acc[bits, rows:, :]


def start(bits, b, a, u, v):
    rows, k = b.shape[0], u.shape[1]
    out = jax.ShapeDtypeStruct((rows, k), jnp.float32)
    return pl.pallas_call(
        functools.partial(start_kernel, bits),
        out_shape=(out, out),
        in_specs=[pl.BlockSpec(memory_space=pl.ANY)] * 4,
        out_specs=(VMEM, VMEM),
        scratch_shapes=[
            pltpu.VMEM(b.shape, jnp.float32),
            pltpu.VMEM(a.shape, jnp.float32),
            pltpu.VMEM(u.shape, jnp.float32),
            pltpu.VMEM(v.shape, jnp.float32),
            pltpu.VMEM((bits + 1, 2 * rows, k), jnp.float32),
            pltpu.VMEM((bits, 2 * rows, k), jnp.float32),
            pltpu.SemaphoreType.DMA((4,)),
            pltpu.SemaphoreType.DMA((2, bits, 2)),
            pltpu.SemaphoreType.DMA((2, bits, 2)),
        ],
        compiler_params=pltpu.CompilerParams(collective_id=0, has_side_effects=True),
    )(b, a, u, v)


def refresh_kernel(bits, chain, rank, f_ref, x_ref, y_ref, m_ref, s_ref, other, pair, up, got, acc, rgot, coeff,
                   pair_send, pair_recv, in_send, recv, out_send, fin_send, fin_recv, row_send, row_recv, gram_send, gram_recv):
    tenant = lax.axis_index("tenant")
    core = lax.rem(tenant, 2)
    place = tenant // 2
    nch = up.shape[0]
    lower = (place < chain // 2).astype(jnp.int32)
    toward = 2 * lower - 1
    mate = {"tenant": tenant + 1 - 2 * core}
    inner = {"tenant": tenant + 2 * toward}
    dist = lower * (chain // 2 - 1 - place) + (1 - lower) * (place - chain // 2)
    mid = (dist == 0).astype(jnp.int32)
    is_end = dist == chain // 2 - 1
    outer = {"tenant": jnp.where(is_end, tenant, tenant - 2 * toward)}

    signal(mate)
    signal(inner)
    for bit in range(bits):
        signal({"row": row_partner(bit)})

    @pl.when(jnp.logical_not(is_end))
    def _():
        signal(outer)

    rows, width = f_ref.shape
    half = width // 2
    tile = up.shape[1]
    block_rows = other.shape[1]
    weight = mm(x_ref[...], x_ref[...], 1, 1)
    same = lax.broadcasted_iota(jnp.int32, weight.shape, 0) // rank == lax.broadcasted_iota(
        jnp.int32, weight.shape, 1) // rank
    coeff[...] = mm(jnp.where(same, weight, 0.0), y_ref[...], 1, 0)
    pl.semaphore_wait(pltpu.get_barrier_semaphore(), 3 + bits - is_end.astype(jnp.int32))

    def rows_of(side, ch):
        return pl.ds(pl.multiple_of(side * half + ch * tile, tile), tile)

    def block_of(side, at):
        return pl.ds(pl.multiple_of(side * half + at * block_rows, block_rows), block_rows)

    def term(side, at):
        return mm3(f_ref[:, block_of(side, at)], coeff[...], 0, 0)

    def pair_copy(at):
        return remote(other.at[at], pair.at[at], pair_send.at[at], pair_recv.at[at], mate)

    def in_copy(ch, slot):
        return remote(up.at[ch], got.at[slot, ch], in_send.at[ch], recv.at[slot, ch], inner)

    def out_copy(ch):
        mine = m_ref.at[rows_of(core, ch)]
        return remote(mine, got.at[1, ch], out_send.at[ch], recv.at[1, ch], outer)

    def fin_copy(side, at):
        part = m_ref.at[block_of(side, at)]
        return remote(part, part, fin_send.at[at], fin_recv.at[at], mate)

    acc[0] = jnp.zeros_like(acc[0])

    def first(ch, _):
        other[ch] = term(1 - core, ch)
        pair_copy(ch).start()
        return 0

    lax.fori_loop(0, nch // 2, first, 0)

    def gather_up(ch):
        at = ch // 2

        @pl.when(lax.rem(ch, 2) == 0)
        def _():
            whole = term(core, at)
            pair_copy(at).wait_recv()
            whole += pair[at]
            up[ch] = whole[:tile]
            up[ch + 1] = whole[tile:]

        @pl.when(jnp.logical_not(is_end))
        def _():
            in_copy(ch, 0).wait_recv()
            up[ch] += got[0, ch]

        in_copy(ch, mid).start()

    k = m_ref.shape[1]
    part = pl.ds(pl.multiple_of(core * (k // 2), k // 2), k // 2)

    def accumulate(at):
        fin_copy(1 - core, at).wait_recv()
        for side in range(2):
            here = block_of(side, at)
            block = m_ref[here, :]
            acc[0, :rows, :] += mm3(f_ref[:, here], block, 1, 0)
            acc[0, rows:, :] += mm(m_ref[here, part], block, 0, 0)

    def settle(ch):
        in_copy(ch, 1).wait_recv()

        @pl.when(mid == 1)
        def _():
            m_ref[rows_of(core, ch), :] = up[ch] + got[1, ch]

        @pl.when(mid == 0)
        def _():
            m_ref[rows_of(core, ch), :] = got[1, ch]

        @pl.when(jnp.logical_not(is_end))
        def _():
            out_copy(ch).start()

        @pl.when(lax.rem(ch, 2) == 1)
        def _():
            fin_copy(core, ch // 2).start()

        @pl.when(jnp.logical_and(lax.rem(ch, 2) == 0, ch > 0))
        def _():
            accumulate(ch // 2 - 1)

    lag = 2 + 5 * dist

    def step(i, _):
        @pl.when(i < nch)
        def _():
            gather_up(i)

        @pl.when(jnp.logical_and(i >= lag, i < nch + lag))
        def _():
            settle(i - lag)

        return 0

    lax.fori_loop(0, nch + 2 + 5 * (chain // 2 - 1), step, 0)
    accumulate(nch // 2 - 1)
    row_sum(bits, acc, rgot, row_send, row_recv)
    s_ref[:rows, :] = acc[bits, :rows, :]

    def gram_copy(side):
        here = s_ref.at[pl.ds(pl.multiple_of(rows + side * (k // 2), 8), k // 2)]
        return remote(here, here, gram_send, gram_recv, mate)

    s_ref[pl.ds(pl.multiple_of(rows + core * (k // 2), 8), k // 2), :] = acc[bits, rows:, :]
    gram_copy(core).start()

    def drain(ch, _):
        in_copy(ch, mid).wait_send()

        @pl.when(ch < nch // 2)
        def _():
            pair_copy(ch).wait_send()
            fin_copy(core, ch).wait_send()

        @pl.when(jnp.logical_not(is_end))
        def _():
            out_copy(ch).wait_send()

        return 0

    lax.fori_loop(0, nch, drain, 0)
    gram_copy(1 - core).wait_recv()
    gram_copy(core).wait_send()


def refresh(bits, chain, rank, f, x, y):
    rows, width = f.shape
    k = x.shape[1]
    wide = min(LANES, width // 2)
    tile = wide // 2
    nch = width // 2 // tile
    f32 = jnp.float32
    dma = pltpu.SemaphoreType.DMA
    return pl.pallas_call(
        functools.partial(refresh_kernel, bits, chain, rank),
        out_shape=(jax.ShapeDtypeStruct((width, k), f32), jax.ShapeDtypeStruct((rows + k, k), f32)),
        in_specs=[VMEM] * 3,
        out_specs=(VMEM, VMEM),
        scratch_shapes=[
            pltpu.VMEM((nch // 2, wide, k), f32),
            pltpu.VMEM((nch // 2, wide, k), f32),
            pltpu.VMEM((nch, tile, k), f32),
            pltpu.VMEM((2, nch, tile, k), f32),
            pltpu.VMEM((bits + 1, rows + k // 2, k), f32),
            pltpu.VMEM((bits, rows + k // 2, k), f32),
            pltpu.VMEM((rows, k), f32),
            dma((nch // 2,)), dma((nch // 2,)), dma((nch,)), dma((2, nch)), dma((nch,)), dma((nch // 2,)),
            dma((nch // 2,)),
            dma((1, bits, 2)), dma((1, bits, 2)), dma(()), dma(()),
        ],
        compiler_params=pltpu.CompilerParams(collective_id=1, has_side_effects=True),
    )(f, x, y)


def factor_block(block):
    n = block.shape[0]
    eye = (lax.broadcasted_iota(jnp.int32, (n, n), 0) == lax.broadcasted_iota(jnp.int32, (n, n), 1)).astype(block.dtype)
    full = jnp.concatenate([block, eye], axis=1)
    groups = [full[8 * g:8 * g + 8, :] for g in range(n // 8)]
    sub = lax.broadcasted_iota(jnp.int32, (8, 2 * n), 0)
    for g in range(n // 8):
        cols = [[jnp.broadcast_to(groups[h][:, 8 * g + c:8 * g + c + 1], (8, 2 * n)) for c in range(8)]
                for h in range(g, n // 8)]
        heads = [[cols[0][c][r:r + 1, :] for c in range(8)] for r in range(8)]
        lines = [groups[g][r:r + 1, :] for r in range(8)]
        invs = []
        for p in range(8):
            inv = 1.0 / heads[p][p]
            invs.append(inv)
            for r in range(p + 1, 8):
                factor = heads[r][p] * inv
                lines[r] = lines[r] - factor * lines[p]
                for c in range(p + 1, 8):
                    heads[r][c] = heads[r][c] - factor * heads[p][c]
        for h in range(g + 1, n // 8):
            col = cols[h - g]
            total = groups[h]
            for p in range(8):
                factor = col[p] * invs[p]
                total = total - factor * lines[p]
                for c in range(p + 1, 8):
                    col[c] = col[c] - factor * heads[p][c]
            groups[h] = total
        group = jnp.broadcast_to(lines[0], (8, 2 * n))
        for r in range(1, 8):
            group = jnp.where(sub == r, lines[r], group)
        groups[g] = group
    full = jnp.concatenate(groups, axis=0)
    diag = jnp.sum(full[:, :n] * eye, axis=1, keepdims=True)
    return full[:, n:] * lax.rsqrt(diag)


def factor_kernel(s_ref, inv_ref, left_ref, tab):
    k = inv_ref.shape[0]
    rows = left_ref.shape[0]
    tab[:, :k] = s_ref[rows:, :]
    tab[:, k:] = (lax.broadcasted_iota(jnp.int32, (k, k), 0) == lax.broadcasted_iota(
        jnp.int32, (k, k), 1)).astype(jnp.float32)
    for at in range(0, k, BLK):
        end = at + BLK
        small = factor_block(tab[at:end, at:end])
        done = mm(small, tab[at:end, :], 1, 0)
        tab[at:end, :] = done
        if end < k:
            tab[end:, :] -= mm(done[:, end:k], done, 0, 0)
    inv_ref[...] = tab[:, k:]
    left_ref[...] = mm(s_ref[:rows, :], tab[:, k:], 1, 1)


def factor(s):
    k = s.shape[1]
    rows = s.shape[0] - k
    return pl.pallas_call(
        factor_kernel,
        out_shape=(jax.ShapeDtypeStruct((k, k), jnp.float32), jax.ShapeDtypeStruct((rows, k), jnp.float32)),
        in_specs=[VMEM],
        out_specs=(VMEM, VMEM),
        scratch_shapes=[pltpu.VMEM((k, 2 * k), jnp.float32)],
    )(s)


def finish(basis, inv):
    return lax.dot_general(basis, inv, (((1,), (1,)), ((), ())), precision=lax.Precision.HIGH)


def local(mesh_shape, b_factors, a_factors, u_start, v_start):
    nt, rank, width = b_factors.shape
    rows = nt * rank
    k = u_start.shape[1]
    bits = bits_of(mesh_shape["row"])
    chain = mesh_shape["tenant"] // 2
    b = b_factors.reshape(rows, width)
    a = a_factors.reshape(rows, width)
    left, right = start(bits, b, a, u_start, v_start)
    basis_u, sums = refresh(bits, chain, rank, b, right, left)
    inv_u, left = factor(sums)
    basis_v, sums = refresh(bits, chain, rank, a, left, right)
    inv_v, right = factor(sums)
    scale = math.sqrt(width * mesh_shape["row"])
    u = finish(basis_u, inv_u * scale)
    v = finish(basis_v, inv_v * scale)
    return u, v, left.reshape(nt, rank, k), right.reshape(nt, rank, k)


def solution(mesh):
    in_specs = (P("tenant", None, "row"), P("tenant", None, "row"), P("row", None), P("row", None))
    out_specs = (P("row", None), P("row", None), P("tenant", None, None), P("tenant", None, None))
    return jax.shard_map(functools.partial(local, dict(mesh.shape)), mesh=mesh, in_specs=in_specs,
                         out_specs=out_specs, check_vma=False)
```

```python
import functools
import math

import jax
import jax.numpy as jnp
from jax import lax
from jax.experimental import pallas as pl
from jax.experimental.pallas import tpu as pltpu
from jax.sharding import PartitionSpec as P

HIGH = lax.Precision.HIGHEST
MESH = pl.DeviceIdType.MESH
VMEM = pl.BlockSpec(memory_space=pltpu.VMEM)
ANY = pl.BlockSpec(memory_space=pl.ANY)
LANES = 128
BLK = 64
OUT = 4


def mm(x, y, cx, cy):
    return lax.dot_general(x, y, (((cx,), (cy,)), ((), ())), precision=HIGH, preferred_element_type=jnp.float32)


def split(x):
    top = x.astype(jnp.bfloat16)
    return top, (x - top.astype(jnp.float32)).astype(jnp.bfloat16)


def mm3(x, y, cx, cy):
    (xt, xl), (yt, yl) = split(x), split(y)
    dot = functools.partial(lax.dot_general, dimension_numbers=(((cx,), (cy,)), ((), ())),
                            preferred_element_type=jnp.float32)
    return dot(xt, yt) + (dot(xt, yl) + dot(xl, yt))


def remote(src, dst, send, recv, device):
    return pltpu.make_async_remote_copy(
        src_ref=src, dst_ref=dst, send_sem=send, recv_sem=recv, device_id=device, device_id_type=MESH)


def signal(device):
    pl.semaphore_signal(pltpu.get_barrier_semaphore(), inc=1, device_id=device, device_id_type=MESH)


def bits_of(n_row):
    bits = n_row.bit_length() - 1
    assert 1 << bits == n_row
    return bits


def row_partner(bit):
    row = lax.axis_index("row")
    return row + (1 << bit) - 2 * (1 << bit) * (lax.rem(row // (1 << bit), 2))


def row_parts(bits, acc, got, send, recv, base, size):
    half = size // 2

    def copy(step, part):
        bit = (step + part) % bits
        rows = pl.ds(base + part * half, half)
        at = base // size
        return remote(acc.at[step, rows], got.at[step, rows], send.at[at, step, part], recv.at[at, step, part],
                      {"row": row_partner(bit)})

    def begin():
        for part in range(2):
            copy(0, part).start()

    def meet(step):
        for part in range(2):
            rows = pl.ds(base + part * half, half)
            copy(step, part).wait_recv()
            acc[step + 1, rows, :] = acc[step, rows, :] + got[step, rows, :]
            if step + 1 < bits:
                copy(step + 1, part).start()

    def end():
        for step in range(bits):
            for part in range(2):
                copy(step, part).wait_send()

    return begin, meet, end


def row_sum(bits, acc, got, send, recv):
    begin, meet, end = row_parts(bits, acc, got, send, recv, 0, acc.shape[1])
    begin()
    for step in range(bits):
        meet(step)
    end()


def start_kernel(bits, b_hbm, a_hbm, u_hbm, v_hbm, left_ref, right_ref, b_ref, a_ref, u_ref, v_ref, acc, got,
                 load, send, recv):
    pairs = ((b_hbm, b_ref), (u_hbm, u_ref), (a_hbm, a_ref), (v_hbm, v_ref))
    loads = [pltpu.make_async_copy(src, dst, load.at[i]) for i, (src, dst) in enumerate(pairs)]
    for copy in loads:
        copy.start()
    for bit in range(bits):
        signal({"row": row_partner(bit)})
    rows, width = b_ref.shape
    tile = 512 if width % 512 == 0 else width
    acc[0] = jnp.zeros_like(acc[0])
    parts = [row_parts(bits, acc, got, send, recv, side * rows, rows) for side in range(2)]
    for side, (factors, basis) in enumerate(((b_ref, u_ref), (a_ref, v_ref))):
        loads[2 * side].wait()
        loads[2 * side + 1].wait()

        def step(i, _, side=side, factors=factors, basis=basis):
            cols = pl.ds(pl.multiple_of(i * tile, tile), tile)
            acc[0, pl.ds(side * rows, rows), :] += mm3(factors[:, cols], basis[cols, :], 1, 0)
            return 0

        lax.fori_loop(0, width // tile, step, 0)
        if side == 0:
            pl.semaphore_wait(pltpu.get_barrier_semaphore(), bits)
        parts[side][0]()
    for step in range(bits):
        for side in range(2):
            parts[side][1](step)
    for side in range(2):
        parts[side][2]()
    left_ref[...] = acc[bits, :rows, :]
    right_ref[...] = acc[bits, rows:, :]


def start(bits, b, a, u, v):
    rows, k = b.shape[0], u.shape[1]
    out = jax.ShapeDtypeStruct((rows, k), jnp.float32)
    return pl.pallas_call(
        functools.partial(start_kernel, bits),
        out_shape=(out, out),
        in_specs=[pl.BlockSpec(memory_space=pl.ANY)] * 4,
        out_specs=(VMEM, VMEM),
        scratch_shapes=[
            pltpu.VMEM(b.shape, jnp.float32),
            pltpu.VMEM(a.shape, jnp.float32),
            pltpu.VMEM(u.shape, jnp.float32),
            pltpu.VMEM(v.shape, jnp.float32),
            pltpu.VMEM((bits + 1, 2 * rows, k), jnp.float32),
            pltpu.VMEM((bits, 2 * rows, k), jnp.float32),
            pltpu.SemaphoreType.DMA((4,)),
            pltpu.SemaphoreType.DMA((2, bits, 2)),
            pltpu.SemaphoreType.DMA((2, bits, 2)),
        ],
        compiler_params=pltpu.CompilerParams(collective_id=0, has_side_effects=True),
    )(b, a, u, v)


def refresh_kernel(bits, chain, rank, f_hbm, x_ref, y_ref, m_hbm, s_ref, f_ref, m_ref, load, store, other, pair, up, got, acc, rgot, coeff,
                   pair_send, pair_recv, in_send, recv, out_send, fin_send, fin_recv, row_send, row_recv, gram_send, gram_recv):
    fetch = pltpu.make_async_copy(f_hbm, f_ref, load)
    fetch.start()
    tenant = lax.axis_index("tenant")
    core = lax.rem(tenant, 2)
    place = tenant // 2
    nch = up.shape[0]
    lower = (place < chain // 2).astype(jnp.int32)
    toward = 2 * lower - 1
    mate = {"tenant": tenant + 1 - 2 * core}
    inner = {"tenant": tenant + 2 * toward}
    dist = lower * (chain // 2 - 1 - place) + (1 - lower) * (place - chain // 2)
    mid = (dist == 0).astype(jnp.int32)
    is_end = dist == chain // 2 - 1
    outer = {"tenant": jnp.where(is_end, tenant, tenant - 2 * toward)}

    signal(mate)
    signal(inner)
    for bit in range(bits):
        signal({"row": row_partner(bit)})

    @pl.when(jnp.logical_not(is_end))
    def _():
        signal(outer)

    rows, width = f_ref.shape
    half = width // 2
    tile = up.shape[1]
    block_rows = other.shape[1]
    weight = mm(x_ref[...], x_ref[...], 1, 1)
    same = lax.broadcasted_iota(jnp.int32, weight.shape, 0) // rank == lax.broadcasted_iota(
        jnp.int32, weight.shape, 1) // rank
    coeff[...] = mm(jnp.where(same, weight, 0.0), y_ref[...], 1, 0)
    pl.semaphore_wait(pltpu.get_barrier_semaphore(), 3 + bits - is_end.astype(jnp.int32))

    def rows_of(side, ch):
        return pl.ds(pl.multiple_of(side * half + ch * tile, tile), tile)

    def block_of(side, at):
        return pl.ds(pl.multiple_of(side * half + at * block_rows, block_rows), block_rows)

    def term(side, at):
        return mm3(f_ref[:, block_of(side, at)], coeff[...], 0, 0)

    def pair_copy(at):
        return remote(other.at[at], pair.at[at], pair_send.at[at], pair_recv.at[at], mate)

    def in_copy(ch, slot):
        return remote(up.at[ch], got.at[slot, ch], in_send.at[ch], recv.at[slot, ch], inner)

    def out_copy(ch):
        mine = m_ref.at[rows_of(core, ch)]
        return remote(mine, got.at[1, ch], out_send.at[ch], recv.at[1, ch], outer)

    def fin_copy(side, at):
        part = m_ref.at[block_of(side, at)]
        return remote(part, part, fin_send.at[at], fin_recv.at[at], mate)

    acc[0] = jnp.zeros_like(acc[0])

    def first(ch, _):
        other[ch] = term(1 - core, ch)
        pair_copy(ch).start()
        return 0

    fetch.wait()
    lax.fori_loop(0, nch // 2, first, 0)

    def gather_up(ch):
        at = ch // 2

        @pl.when(lax.rem(ch, 2) == 0)
        def _():
            whole = term(core, at)
            pair_copy(at).wait_recv()
            whole += pair[at]
            up[ch] = whole[:tile]
            up[ch + 1] = whole[tile:]

        @pl.when(jnp.logical_not(is_end))
        def _():
            in_copy(ch, 0).wait_recv()
            up[ch] += got[0, ch]

        in_copy(ch, mid).start()

    k = m_ref.shape[1]
    part = pl.ds(pl.multiple_of(core * (k // 2), k // 2), k // 2)

    def keep(side, at):
        here = block_of(side, at)
        return pltpu.make_async_copy(m_ref.at[here], m_hbm.at[here], store.at[side, at])

    def accumulate(at):
        fin_copy(1 - core, at).wait_recv()
        for side in range(2):
            here = block_of(side, at)
            keep(side, at).start()
            block = m_ref[here, :]
            acc[0, :rows, :] += mm3(f_ref[:, here], block, 1, 0)
            acc[0, rows:, :] += mm(m_ref[here, part], block, 0, 0)

    def settle(ch):
        in_copy(ch, 1).wait_recv()

        @pl.when(mid == 1)
        def _():
            m_ref[rows_of(core, ch), :] = up[ch] + got[1, ch]

        @pl.when(mid == 0)
        def _():
            m_ref[rows_of(core, ch), :] = got[1, ch]

        @pl.when(jnp.logical_not(is_end))
        def _():
            out_copy(ch).start()

        @pl.when(lax.rem(ch, 2) == 1)
        def _():
            fin_copy(core, ch // 2).start()

        @pl.when(jnp.logical_and(lax.rem(ch, 2) == 0, ch > 0))
        def _():
            accumulate(ch // 2 - 1)

    lag = 2 + 5 * dist

    def step(i, _):
        @pl.when(i < nch)
        def _():
            gather_up(i)

        @pl.when(jnp.logical_and(i >= lag, i < nch + lag))
        def _():
            settle(i - lag)

        return 0

    lax.fori_loop(0, nch + 2 + 5 * (chain // 2 - 1), step, 0)
    accumulate(nch // 2 - 1)
    row_sum(bits, acc, rgot, row_send, row_recv)
    s_ref[:rows, :] = acc[bits, :rows, :]

    def gram_copy(side):
        here = s_ref.at[pl.ds(pl.multiple_of(rows + side * (k // 2), 8), k // 2)]
        return remote(here, here, gram_send, gram_recv, mate)

    s_ref[pl.ds(pl.multiple_of(rows + core * (k // 2), 8), k // 2), :] = acc[bits, rows:, :]
    gram_copy(core).start()

    def drain(ch, _):
        in_copy(ch, mid).wait_send()

        @pl.when(ch < nch // 2)
        def _():
            pair_copy(ch).wait_send()
            fin_copy(core, ch).wait_send()
            for side in range(2):
                keep(side, ch).wait()

        @pl.when(jnp.logical_not(is_end))
        def _():
            out_copy(ch).wait_send()

        return 0

    lax.fori_loop(0, nch, drain, 0)
    gram_copy(1 - core).wait_recv()
    gram_copy(core).wait_send()


def refresh(bits, chain, rank, f, x, y):
    rows, width = f.shape
    k = x.shape[1]
    wide = min(LANES, width // 2)
    tile = wide // 2
    nch = width // 2 // tile
    f32 = jnp.float32
    dma = pltpu.SemaphoreType.DMA
    return pl.pallas_call(
        functools.partial(refresh_kernel, bits, chain, rank),
        out_shape=(jax.ShapeDtypeStruct((width, k), f32), jax.ShapeDtypeStruct((rows + k, k), f32)),
        in_specs=[ANY, VMEM, VMEM],
        out_specs=(ANY, VMEM),
        scratch_shapes=[
            pltpu.VMEM((rows, width), f32),
            pltpu.VMEM((width, k), f32),
            dma(()), dma((2, nch // 2)),
            pltpu.VMEM((nch // 2, wide, k), f32),
            pltpu.VMEM((nch // 2, wide, k), f32),
            pltpu.VMEM((nch, tile, k), f32),
            pltpu.VMEM((2, nch, tile, k), f32),
            pltpu.VMEM((bits + 1, rows + k // 2, k), f32),
            pltpu.VMEM((bits, rows + k // 2, k), f32),
            pltpu.VMEM((rows, k), f32),
            dma((nch // 2,)), dma((nch // 2,)), dma((nch,)), dma((2, nch)), dma((nch,)), dma((nch // 2,)),
            dma((nch // 2,)),
            dma((1, bits, 2)), dma((1, bits, 2)), dma(()), dma(()),
        ],
        compiler_params=pltpu.CompilerParams(collective_id=1, has_side_effects=True),
    )(f, x, y)


def factor_block(block):
    n = block.shape[0]
    eye = (lax.broadcasted_iota(jnp.int32, (n, n), 0) == lax.broadcasted_iota(jnp.int32, (n, n), 1)).astype(block.dtype)
    full = jnp.concatenate([block, eye], axis=1)
    groups = [full[8 * g:8 * g + 8, :] for g in range(n // 8)]
    sub = lax.broadcasted_iota(jnp.int32, (8, 2 * n), 0)
    for g in range(n // 8):
        cols = [[jnp.broadcast_to(groups[h][:, 8 * g + c:8 * g + c + 1], (8, 2 * n)) for c in range(8)]
                for h in range(g, n // 8)]
        heads = [[cols[0][c][r:r + 1, :] for c in range(8)] for r in range(8)]
        lines = [groups[g][r:r + 1, :] for r in range(8)]
        invs = []
        for p in range(8):
            inv = 1.0 / heads[p][p]
            invs.append(inv)
            for r in range(p + 1, 8):
                factor = heads[r][p] * inv
                lines[r] = lines[r] - factor * lines[p]
                for c in range(p + 1, 8):
                    heads[r][c] = heads[r][c] - factor * heads[p][c]
        for h in range(g + 1, n // 8):
            col = cols[h - g]
            total = groups[h]
            for p in range(8):
                factor = col[p] * invs[p]
                total = total - factor * lines[p]
                for c in range(p + 1, 8):
                    col[c] = col[c] - factor * heads[p][c]
            groups[h] = total
        group = jnp.broadcast_to(lines[0], (8, 2 * n))
        for r in range(1, 8):
            group = jnp.where(sub == r, lines[r], group)
        groups[g] = group
    full = jnp.concatenate(groups, axis=0)
    diag = jnp.sum(full[:, :n] * eye, axis=1, keepdims=True)
    return full[:, n:] * lax.rsqrt(diag)


def factor_kernel(scale, s_ref, m_hbm, out_hbm, left_ref, tab, m_ref, out_ref, load, store):
    fetch = pltpu.make_async_copy(m_hbm, m_ref, load)
    fetch.start()
    k = s_ref.shape[1]
    rows = left_ref.shape[0]
    tab[:, :k] = s_ref[rows:, :]
    tab[:, k:] = (lax.broadcasted_iota(jnp.int32, (k, k), 0) == lax.broadcasted_iota(
        jnp.int32, (k, k), 1)).astype(jnp.float32)
    for at in range(0, k, BLK):
        end = at + BLK
        small = factor_block(tab[at:end, at:end])
        done = mm(small, tab[at:end, :], 1, 0)
        tab[at:end, :] = done
        if end < k:
            tab[end:, :] -= mm(done[:, end:k], done, 0, 0)
    left_ref[...] = mm(s_ref[:rows, :], tab[:, k:], 1, 1)
    scaled = tab[:, k:] * scale
    fetch.wait()
    size = m_ref.shape[0] // OUT
    copies = []
    for i in range(OUT):
        here = pl.ds(i * size, size)
        out_ref[here, :] = mm3(m_ref[here, :], scaled, 1, 1)
        copies.append(pltpu.make_async_copy(out_ref.at[here], out_hbm.at[here], store.at[i]))
        copies[-1].start()
    for copy in copies:
        copy.wait()


def factor(scale, s, m):
    k = s.shape[1]
    rows = s.shape[0] - k
    return pl.pallas_call(
        functools.partial(factor_kernel, scale),
        out_shape=(jax.ShapeDtypeStruct(m.shape, jnp.float32), jax.ShapeDtypeStruct((rows, k), jnp.float32)),
        in_specs=[VMEM, ANY],
        out_specs=(ANY, VMEM),
        scratch_shapes=[
            pltpu.VMEM((k, 2 * k), jnp.float32),
            pltpu.VMEM(m.shape, jnp.float32),
            pltpu.VMEM(m.shape, jnp.float32),
            pltpu.SemaphoreType.DMA(()),
            pltpu.SemaphoreType.DMA((OUT,)),
        ],
    )(s, m)


def local(mesh_shape, b_factors, a_factors, u_start, v_start):
    nt, rank, width = b_factors.shape
    rows = nt * rank
    k = u_start.shape[1]
    bits = bits_of(mesh_shape["row"])
    chain = mesh_shape["tenant"] // 2
    b = b_factors.reshape(rows, width)
    a = a_factors.reshape(rows, width)
    left, right = start(bits, b, a, u_start, v_start)
    scale = math.sqrt(width * mesh_shape["row"])
    basis_u, sums = refresh(bits, chain, rank, b, right, left)
    u, left = factor(scale, sums, basis_u)
    basis_v, sums = refresh(bits, chain, rank, a, left, right)
    v, right = factor(scale, sums, basis_v)
    return u, v, left.reshape(nt, rank, k), right.reshape(nt, rank, k)


def solution(mesh):
    in_specs = (P("tenant", None, "row"), P("tenant", None, "row"), P("row", None), P("row", None))
    out_specs = (P("row", None), P("row", None), P("tenant", None, None), P("tenant", None, None))
    return jax.shard_map(functools.partial(local, dict(mesh.shape)), mesh=mesh, in_specs=in_specs,
                         out_specs=out_specs, check_vma=False)
```
